128 devices in a mesh: section: 2 (over core), cin: 8 (over z_hi, y), cout: 8 (over z_lo, x).
Axes of the slice: x: 4, y: 4, z: 4 (z_hi: 2, z_lo: 2; z = z_hi * 2 + z_lo), core: 2. Of those that a mesh axis runs over, the one named last changes fastest.
Arguments:
- inner_features: bfloat16 [2, 784, 2560], P('section', None, ('cin', 'cout')), may hold values from 0 to 2
- block_input: bfloat16 [2, 784, 5120], P('section', None, ('cin', 'cout')), may hold values from -6 to 6
- first_kernel: bfloat16 [9, 2560, 2560], P(None, 'cin', 'cout'), may hold values from -0.0546875 to 0.0546875
- expand_weight: bfloat16 [2560, 5120], P('cout', 'cin'), may hold values from -0.15625 to 0.15625
- reduce_weight: bfloat16 [5120, 5120], P(('cin', 'section'), 'cout'), may hold values from -0.125 to 0.125
- stride_kernel: bfloat16 [9, 5120, 5120], P(None, 'cout', ('section', 'cin')), may hold values from -0.0390625 to 0.0390625
- output_grad: bfloat16 [2, 196, 5120], P(None, None, ('section', 'cin', 'cout')), may hold values from -6 to 6
Outputs:
- inner_gradient: float32 [2, 784, 2560], P('section', None, ('cin', 'cout'))
- input_gradient: bfloat16 [2, 784, 5120], P('section', None, ('cin', 'cout'))
- first_gradient: float32 [9, 2560, 2560], P(None, 'cin', 'cout')
- expand_gradient: float32 [2560, 5120], P('cout', 'cin')
- reduce_gradient: float32 [5120, 5120], P(('cin', 'section'), 'cout')
- stride_gradient: float32 [9, 5120, 5120], P(None, 'cout', ('section', 'cin'))
The draws below stay inside these ranges and needn't reach their ends.
All inputs are finite; a program needn't handle non-finite values.
Results may differ from the reference program's by a relative error of at most 0.013.
Values may be sent and summed in bfloat16 or wider, within the bound.
A program may use at most 192 MiB of HBM per device.

```python
import jax
import jax.numpy as jnp
from jax import lax

INA = 2560
OUTA = 5120
INB = 5120
SIDE = 28
IMAGES = 2
HW = 784
HH = 196


def raised(values, own_key, source, target, blocks, factor):
    def block_of(axis_at):
        return (jnp.arange(values.shape[axis_at]) // (values.shape[axis_at] // blocks)).reshape((-1,) + (1,) * (values.ndim - 1 - axis_at))

    near = jax.random.permutation(own_key, blocks)[block_of(target)]
    other_side = (block_of(target) + blocks // 2) % blocks
    return jnp.where((block_of(source) == near) | (block_of(source) == other_side), factor * values, values)


def shard_levels(rng, extent, shards, low, top_value):
    gain = 1.0
    for axis_at, parts in shards:
        heights = jax.random.uniform(jax.random.fold_in(jax.random.fold_in(rng, 6), axis_at), (parts,), jnp.float32, low / len(shards), top_value / len(shards))
        gain = gain * jnp.repeat(jnp.exp(heights), extent[axis_at] // parts).reshape((-1,) + (1,) * (len(extent) - 1 - axis_at))
    return gain


def gaussian(own_key, shape, spread, bound, pieces=(), kind=jnp.bfloat16):
    values = jax.random.normal(own_key, shape, jnp.float32) * spread
    if len(pieces) > 0:
        values = shard_levels(own_key, shape, pieces, -0.22, 0.18) * values
    return jnp.clip(values, min=-bound, max=bound).astype(kind)


def bell_draw_with(own_key, dims, deviation, bound, split, heavy, kind=jnp.bfloat16):
    drawn = deviation * jax.random.normal(own_key, dims, jnp.float32)
    if split:
        drawn = drawn * shard_levels(own_key, dims, split, -0.22, 0.18)
    return jnp.clip(raised(drawn, jax.random.fold_in(own_key, 3), *heavy), -bound, bound).astype(kind)


def setup_inputs(seed: int = 0) -> dict:
    splits = jax.random.split(jax.random.key(seed), 8)
    inner_features = jnp.clip(2.0 * jax.random.uniform(splits[0], (IMAGES, HW, INA), jnp.float32) ** shard_levels(splits[0], (IMAGES, HW, INA), ((0, 2), (2, 64)), -0.2, 0.2), 0.0, 2.0).astype(jnp.bfloat16)
    block_input = gaussian(splits[1], (IMAGES, HW, OUTA), 1.0, 6.0, ((0, 2), (2, 64)))
    first_kernel = bell_draw_with(splits[2], (9, INA, INA), (9 * INA) ** -0.5, 0.0546875, ((1, 8), (2, 8)), (1, 2, 8, 2.0))
    expand_weight = bell_draw_with(splits[3], (INA, OUTA), INA ** -0.5, 0.15625, ((0, 8), (1, 8)), (0, 1, 8, 2.0))
    reduce_weight = bell_draw_with(splits[4], (OUTA, INB), OUTA ** -0.5, 0.125, ((0, 16), (1, 8)), (0, 1, 16, 2.0))
    stride_kernel = bell_draw_with(splits[5], (9, INB, INB), (9 * INB) ** -0.5, 0.0390625, ((1, 8), (2, 16)), (2, 1, 16, 2.0))
    output_grad = gaussian(splits[6], (IMAGES, HH, INB), 1.0, 6.0, ((2, 128),))
    return {"inner_features": inner_features, "block_input": block_input, "first_kernel": first_kernel, "expand_weight": expand_weight, "reduce_weight": reduce_weight, "stride_kernel": stride_kernel, "output_grad": output_grad}


def smooth_gate(values):
    return values * jax.nn.sigmoid(values)


def gate_slope(values):
    logistic = jax.nn.sigmoid(values)
    return logistic * (1.0 + values * (1.0 - logistic))


def flatten_rows(images):
    return images.reshape(images.shape[0] * images.shape[1], images.shape[2])


def project(images, matrix):
    product = jnp.dot(flatten_rows(images), matrix, preferred_element_type=jnp.float32)
    return product.reshape(images.shape[0], images.shape[1], matrix.shape[1])


def project_back(grads, matrix):
    product = lax.dot_general(flatten_rows(grads), matrix, (((1,), (1,)), ((), ())), preferred_element_type=jnp.float32)
    return product.reshape(grads.shape[0], grads.shape[1], matrix.shape[0])


def outer_rows(left, right):
    return lax.dot_general(flatten_rows(left), flatten_rows(right), (((0,), (0,)), ((), ())), preferred_element_type=jnp.float32)


def padded_grid(images, side):
    grid = images.reshape(images.shape[0], side, side, images.shape[2])
    return jnp.pad(grid, ((0, 0), (1, 1), (1, 1), (0, 0)))


def conv_same(images, kernel, side):
    padded = padded_grid(images, side)
    total = jnp.zeros((images.shape[0] * side * side, kernel.shape[2]), jnp.float32)
    for row in range(3):
        for column in range(3):
            window = padded[:, row:row + side, column:column + side, :].reshape(-1, images.shape[2])
            total = total + jnp.dot(window, kernel[3 * row + column], preferred_element_type=jnp.float32)
    return total.reshape(images.shape[0], side * side, kernel.shape[2])


def conv_same_back(grads, kernel, side):
    padded = padded_grid(grads, side)
    total = jnp.zeros((grads.shape[0] * side * side, kernel.shape[1]), jnp.float32)
    for row in range(3):
        for column in range(3):
            window = padded[:, 2 - row:2 - row + side, 2 - column:2 - column + side, :].reshape(-1, grads.shape[2])
            total = total + lax.dot_general(window, kernel[3 * row + column], (((1,), (1,)), ((), ())), preferred_element_type=jnp.float32)
    return total.reshape(grads.shape[0], side * side, kernel.shape[1])


def conv_same_weight(images, grads, side):
    padded = padded_grid(images, side)
    flat = flatten_rows(grads)
    terms = []
    for row in range(3):
        for column in range(3):
            window = padded[:, row:row + side, column:column + side, :].reshape(-1, images.shape[2])
            terms.append(lax.dot_general(window, flat, (((0,), (0,)), ((), ())), preferred_element_type=jnp.float32))
    return jnp.stack(terms)


def conv_half_back(grads, kernel, side):
    half = side // 2
    count = grads.shape[0]
    flat = flatten_rows(grads)
    canvas = None
    for row in range(3):
        for column in range(3):
            term = lax.dot_general(flat, kernel[3 * row + column], (((1,), (1,)), ((), ())), preferred_element_type=jnp.float32)
            term = term.reshape(count, half, half, kernel.shape[1])
            placed = lax.pad(term, jnp.zeros((), term.dtype), ((0, 0, 0), (row, 3 - row, 1), (column, 3 - column, 1), (0, 0, 0)))
            canvas = placed if canvas is None else canvas + placed
    return canvas[:, 1:side + 1, 1:side + 1, :].reshape(count, side * side, kernel.shape[1])


def conv_half_weight(images, grads, side):
    padded = padded_grid(images, side)
    flat = flatten_rows(grads)
    terms = []
    for row in range(3):
        for column in range(3):
            window = padded[:, row:row + side:2, column:column + side:2, :].reshape(-1, images.shape[2])
            terms.append(lax.dot_general(window, flat, (((0,), (0,)), ((), ())), preferred_element_type=jnp.float32))
    return jnp.stack(terms)


def reference(inner_features, block_input, first_kernel, expand_weight, reduce_weight, stride_kernel, output_grad):
    first_hidden = conv_same(inner_features, first_kernel, SIDE)
    first_act = smooth_gate(first_hidden).astype(jnp.bfloat16)
    expanded = project(first_act, expand_weight)
    joined_pre = block_input.astype(jnp.float32) + expanded
    joined = smooth_gate(joined_pre).astype(jnp.bfloat16)
    second_hidden = project(joined, reduce_weight)
    second_act = smooth_gate(second_hidden).astype(jnp.bfloat16)
    back_second = conv_half_back(output_grad, stride_kernel, SIDE)
    stride_gradient = conv_half_weight(second_act, output_grad, SIDE)
    masked_second = (back_second * gate_slope(second_hidden)).astype(jnp.bfloat16)
    reduce_gradient = outer_rows(joined, masked_second)
    back_joined = project_back(masked_second, reduce_weight)
    input_gradient = (back_joined * gate_slope(joined_pre)).astype(jnp.bfloat16)
    expand_gradient = outer_rows(first_act, input_gradient)
    back_first = project_back(input_gradient, expand_weight)
    masked_first = (back_first * gate_slope(first_hidden)).astype(jnp.bfloat16)
    inner_gradient = conv_same_back(masked_first, first_kernel, SIDE)
    first_gradient = conv_same_weight(inner_features, masked_first, SIDE)
    return (inner_gradient, input_gradient, first_gradient, expand_gradient, reduce_gradient, stride_gradient)
```

```python
import functools

import jax
import jax.numpy as jnp
import numpy as np
from jax import lax
from jax.experimental import pallas as pl
from jax.experimental.pallas import tpu as pltpu
from jax.sharding import PartitionSpec as P

MESH = pl.DeviceIdType.MESH
BF = jnp.bfloat16
F32 = jnp.float32

SIDE = 28
HALF = 14
PIX = 896
PLANE = 224
LANES = 128
TALL = 48
CHUNKS = 7
HALVES = ((0, 512), (512, 384))


def sigmoid(v):
    return 1.0 / (1.0 + jnp.exp(-v))


def gate(v):
    return v * sigmoid(v)


def slope(v):
    s = sigmoid(v)
    return s * (1.0 + v * (1.0 - s))


def parity_index():
    y, x = np.divmod(np.arange(SIDE * SIDE), SIDE)
    return ((y % 2) * 2 + x % 2) * PLANE + (y // 2) * 16 + x // 2


def natural_index():
    y, x = np.divmod(np.arange(SIDE * SIDE), SIDE)
    return y * 32 + x


def one_hot(rows, columns, shape):
    out = np.zeros(shape, np.float32)
    out[rows, columns] = 1.0
    return out


def place_natural():
    return one_hot(np.arange(SIDE * SIDE), natural_index(), (SIDE * SIDE, PIX))


def place_parity():
    return one_hot(np.arange(SIDE * SIDE), parity_index(), (SIDE * SIDE, PIX))


def natural_to_parity():
    return one_hot(natural_index(), parity_index(), (PIX, PIX))


def place_grad():
    a, b = np.divmod(np.arange(HALF * HALF), HALF)
    return one_hot(np.arange(HALF * HALF), a * 16 + b, (HALF * HALF, 256))


RANGES = ((0, 256), (128, 384), (384, 384), (640, 256))
PLANE_TAPS = (
    ((4, 0, 0),),
    ((5, 0, 0), (3, 0, 1)),
    ((7, 0, 0), (1, 1, 0)),
    ((8, 0, 0), (6, 0, 1), (2, 1, 0), (0, 1, 1)),
)


def tap_table():
    table, at = [], 0
    for plane, taps in enumerate(PLANE_TAPS):
        for tap, _, _ in taps:
            table.append((plane, tap, at))
            at += RANGES[plane][1]
    return table, at


TAPS, PLACED = tap_table()


def spread_grad():
    out = np.zeros((256, PLACED), np.float32)
    entry = 0
    for plane, taps in enumerate(PLANE_TAPS):
        for _, sy, sx in taps:
            at = TAPS[entry][2] + plane * PLANE - RANGES[plane][0]
            entry += 1
            for a in range(HALF - sy):
                for b in range(HALF - sx):
                    out[(a + sy) * 16 + b + sx, at + a * 16 + b] = 1.0
    return out


def signal(devices):
    barrier = pltpu.get_barrier_semaphore()
    for device in devices:
        pl.semaphore_signal(barrier, inc=1, device_id=device, device_id_type=MESH)
    return lambda: pl.semaphore_wait(barrier, len(devices))


def started(src, dst, sem):
    copy = pltpu.make_async_copy(src, dst, sem)
    copy.start()
    return copy


def remote(src, dst, send, recv, device):
    return pltpu.make_async_remote_copy(
        src_ref=src, dst_ref=dst, send_sem=send, recv_sem=recv, device_id=device, device_id_type=MESH
    )


def rows_at(block, size):
    return pl.ds(pl.multiple_of(block * size, size), size)


def others(axis, size=8):
    me = lax.axis_index(axis)
    return [lax.rem(me + d, size) for d in range(1, size)]


def call(body, outs, scratch, collective_id, *args, far_in=(), far_out=()):
    near, far = pl.BlockSpec(memory_space=pltpu.VMEM), pl.BlockSpec(memory_space=pl.ANY)
    return pl.pallas_call(
        body,
        out_shape=tuple(jax.ShapeDtypeStruct(s, d) for s, d in outs),
        in_specs=[far if n in far_in else near for n in range(len(args))],
        out_specs=tuple(far if n in far_out else near for n in range(len(outs))),
        scratch_shapes=scratch,
        compiler_params=pltpu.CompilerParams(
            collective_id=collective_id, has_side_effects=True, vmem_limit_bytes=56 * 2**20
        ),
    )(*args)


def dot(left, right, contract, kind=F32):
    return lax.dot_general(left, right, (contract, ((), ())), preferred_element_type=F32).astype(kind)


NN = ((1,), (0,))
TN = ((0,), (0,))
NT = ((1,), (1,))


def patches_of(x_ref, out_ref, wide):
    size = x_ref.shape[0]
    lane = lax.broadcasted_iota(jnp.int32, (1, PIX), 1)
    for tx in range(3):
        dx = tx - 1
        wide[...] = pltpu.roll(x_ref[...], (PIX - dx) % PIX, 1) if dx else x_ref[...]
        for ty in range(3):
            dy = ty - 1
            at = (3 * ty + tx) * size
            if dy:
                moved = pltpu.roll(wide[...], (PIX - 32 * dy) % PIX, 1)
                keep = (lane + 32 * dy >= 0) & (lane + 32 * dy < PIX)
                out_ref[at : at + size, :] = jnp.where(keep, moved, 0.0).astype(BF)
            else:
                out_ref[at : at + size, :] = wide[...].astype(BF)


def gather_phase(
    met, feature_ref, grads_ref, natural_ref, spot_ref, patches_ref, patches_save, grad_ref, own, grads_own, gathered,
    grads_gathered, grid, wide, send, recv,
):
    me = lax.axis_index("cout")
    narrow, size = feature_ref.shape[0], own.shape[0]
    own[...] = jnp.concatenate(
        [dot(feature_ref[...], natural_ref[...], NN), jnp.zeros((size - narrow, PIX), F32)], axis=0
    ).astype(BF)
    placed = [dot(grads_ref[image], spot_ref[...], NN) for image in range(2)]
    grads_own[...] = jnp.concatenate(
        [jnp.concatenate(placed, axis=1), jnp.zeros((size - narrow, 512), F32)], axis=0
    ).astype(BF)
    met()
    copies = []
    for n, (source, target) in enumerate(((own, gathered), (grads_own, grads_gathered))):
        for d, peer in enumerate(others("cout")):
            copy = remote(
                source, target.at[rows_at(me, size)], send.at[7 * n + d], recv.at[7 * n + d], {"cout": peer}
            )
            copy.start()
            copies.append(copy)
        target[rows_at(me, size), :] = source[...]
    for copy in copies[:7]:
        copy.wait_recv()
    for j in range(8):
        grid[j * narrow : (j + 1) * narrow, :] = gathered[j * size : (j + 1) * size, :].astype(F32)[:narrow]
    patches_of(grid, patches_ref, wide)
    patches_save.start()

    def cotangent():
        for copy in copies[7:]:
            copy.wait_recv()
        for j in range(8):
            block = grads_gathered[j * size : (j + 1) * size, :].astype(F32)
            wide[j * narrow : (j + 1) * narrow, :512] = block[:narrow]
        for image in range(2):
            grad_ref[image] = wide[:, image * 256 : (image + 1) * 256].astype(BF)
        for copy in copies:
            copy.wait_send()

    return cotangent


def inner_exchange(met, prepare, part_of, finish, fill, out_ref, sbuf, rbuf, sems):
    send, recv, send2, recv2 = sems
    me = lax.axis_index("cin")
    peers = others("cin")
    rows = [slice(0, LANES), slice(LANES, out_ref.shape[0])]
    spot = lax.rem(me, CHUNKS)
    first, second = {}, {}
    for h in range(2):
        prepare(rows[h])
        if h == 0:
            met()
        for d, peer in enumerate(peers):
            n = 7 * h + d
            first[h, d] = remote(
                sbuf.at[peer, rows[h]], rbuf.at[d, rows[h]], send.at[n], recv.at[n], {"cin": peer}
            )
            second[h, d] = remote(
                sbuf.at[7, rows[h]], out_ref.at[rows[h], rows_at(spot, LANES)], send2.at[n], recv2.at[n], {"cin": peer}
            )

            @pl.when(peer < CHUNKS)
            def _(h=h, d=d, peer=peer):
                sbuf[peer, rows[h]] = part_of(peer, rows[h]).astype(BF)
                first[h, d].start()

    fill(0)

    @pl.when(me < CHUNKS)
    def _():
        for h in range(2):
            total = part_of(me, rows[h])
            for d in range(7):
                first[h, d].wait_recv()
                total = total + rbuf[d, rows[h]].astype(F32)
            result = finish(total, rows[h])
            sbuf[7, rows[h]] = result
            for d in range(7):
                second[h, d].start()
            out_ref[rows[h], rows_at(me, LANES)] = result

    fill(1)
    for d in range(7):
        source = lax.rem(me + 7 - d, 8)

        @pl.when(source < CHUNKS)
        def _(d=d):
            for h in range(2):
                second[h, d].wait_recv()

    for d, peer in enumerate(peers):

        @pl.when(peer < CHUNKS)
        def _(d=d):
            for h in range(2):
                first[h, d].wait_send()

    @pl.when(me < CHUNKS)
    def _():
        for copy in second.values():
            copy.wait_send()


def nothing():
    pass


def column():
    line = lax.axis_index("cin")
    base, y = line // 4 * 4, lax.rem(line, 4)
    return [base + lax.rem(y + d, 4) for d in range(1, 4)], lax.rem(line + 4, 8)


def all_outer():
    me, core = lax.axis_index("cout"), lax.axis_index("section")
    out = [{"section": 1 - core, "cout": me}]
    for peer in others("cout"):
        out.append({"section": core, "cout": peer})
        out.append({"section": 1 - core, "cout": peer})
    return out


def joined_phase(
    act_ref, parity_ref, weight_ref, input_ref, place_ref, place_load, back_ref, joined_ref, pre_ref, backsum_ref,
    moved_ref, part, sbuf, rbuf, own, pbuf, bsend, brecv, tsend, trecv, send, recv, send2, recv2, psem, qsem, send3,
    recv3,
):
    me, core = lax.axis_index("cout"), lax.axis_index("section")
    line = lax.axis_index("cin")
    rows = input_ref.shape[0]
    peers = others("cout")
    column_peers, across = column()
    pair = remote(back_ref.at[1 - core], pbuf, psem, qsem, {"section": 1 - core, "cout": me})
    pair.start()
    first = {}
    for h, (at, size) in enumerate(HALVES):
        span = slice(at, at + size)
        moved_ref[:, span] = dot(act_ref[...], parity_ref[:, span], NN, BF)
        part[:, span] = dot(weight_ref[...], moved_ref[:, span], TN)
        for d, peer in enumerate(peers):
            sbuf[d, :, span] = part[rows_at(peer, rows), span].astype(BF)
            first[h, d] = remote(
                sbuf.at[d, :, span], rbuf.at[d, :, span], send.at[7 * h + d], recv.at[7 * h + d], {"cout": peer}
            )
            first[h, d].start()
    pair.wait_recv()

    def both(at):
        return back_ref[core, at, :].astype(F32) + pbuf[at, :].astype(F32)

    y, z = lax.rem(line, 4), line // 4
    third = []
    for d, peer in enumerate(column_peers):
        for q in range(2):
            bsend[d, q] = both(rows_at(q * 4 + lax.rem(peer, 4), rows)).astype(BF)
        copy = remote(bsend.at[d], brecv.at[d], send3.at[d], recv3.at[d], {"cin": peer})
        copy.start()
        third.append(copy)
    place_load.wait()
    pre_ref[...] = dot(input_ref[...], place_ref[...], NN) + part[rows_at(me, rows), :]
    target, place = me // 4, lax.rem(me, 4)
    slot = core * 4 + place
    second = {}
    for h, (at, size) in enumerate(HALVES):
        span = slice(at, at + size)
        total = pre_ref[:, span]
        for d in range(7):
            first[h, d].wait_recv()
            total = total + rbuf[d, :, span].astype(F32)
        pre_ref[:, span] = total
        own[:, span] = gate(total).astype(BF)
        lanes = pl.ds(pl.multiple_of(core * PIX + at, LANES), size)
        for d in range(8):
            copy = remote(
                own.at[:, span],
                joined_ref.at[rows_at(place, rows), lanes],
                send2.at[8 * h + d],
                recv2.at[8 * h + slot],
                {"section": target, "cout": lax.rem(me + d, 8)},
            )
            second[h, d] = copy
            if d:
                copy.start()
            else:

                @pl.when(target != core)
                def _(copy=copy):
                    copy.start()

                @pl.when(target == core)
                def _(span=span, lanes=lanes):
                    joined_ref[rows_at(place, rows), lanes] = own[:, span]

    for d in range(3):
        third[d].wait_recv()

    def column_sum(q):
        value = both(rows_at(q * 4 + y, rows))
        for d in range(3):
            value = value + brecv[d, q].astype(F32)
        return value

    tsend[...] = column_sum(1 - z).astype(BF)
    third.append(remote(tsend, trecv, send3.at[3], recv3.at[3], {"cin": across}))
    third[3].start()
    backsum_ref[...] = column_sum(z)
    for h, (at, size) in enumerate(HALVES):
        for image in range(2):
            for k in range(4):
                mine = (core == image) & (me == core * 4 + k)
                arrival = remote(
                    own.at[:, at : at + size],
                    joined_ref.at[k * rows : (k + 1) * rows, image * PIX + at : image * PIX + at + size],
                    send2.at[0],
                    recv2.at[8 * h + image * 4 + k],
                    {"section": core, "cout": me},
                )

                @pl.when(jnp.logical_not(mine))
                def _(arrival=arrival):
                    arrival.wait_recv()

    third[3].wait_recv()
    backsum_ref[...] = backsum_ref[...] + trecv[...].astype(F32)
    pair.wait_send()
    for copy in third:
        copy.wait_send()
    for h in range(2):
        for d in range(7):
            first[h, d].wait_send()
            second[h, d + 1].wait_send()

        @pl.when(target != core)
        def _(h=h):
            second[h, 0].wait_send()


def front_body(
    feature_ref, grads_ref, natural_ref, spot_ref, kernel_far, spread_far, stride_far, parity_far, weight_ref, input_ref,
    place_far, patches_far, hidden_ref, placed_far, joined_ref, pre_ref, backsum_ref, moved_ref,
    own, grads_own, gathered, grads_gathered, grid, wide, kernel_ref, patches_ref, part_ref, grad_ref, spread_ref, stride_ref, placed_ref, back_ref,
    total_ref, parity_ref, place_ref, act_ref, local, gsend, grecv, isbuf, irbuf, isend, irecv, isend2, irecv2, *joins,
):
    met = signal(all_outer() + [{"cin": p} for p in others("cin")])
    loads = [
        started(far, near, local.at[n])
        for n, (far, near) in enumerate(
            (
                (kernel_far, kernel_ref),
                (spread_far, spread_ref),
                (stride_far, stride_ref),
                (parity_far, parity_ref),
                (place_far, place_ref),
            )
        )
    ]
    saves = [
        pltpu.make_async_copy(patches_ref, patches_far, local.at[5]),
        pltpu.make_async_copy(placed_ref, placed_far, local.at[6]),
    ]
    cotangent = gather_phase(
        met, feature_ref, grads_ref, natural_ref, spot_ref, patches_ref, saves[0], grad_ref, own, grads_own, gathered,
        grads_gathered, grid, wide, gsend, grecv,
    )
    loads[0].wait()

    @pl.when(lax.axis_index("cin") == CHUNKS)
    def _():
        hidden_ref[...] = jnp.zeros_like(hidden_ref)

    def fill(stage):
        if stage == 0:
            cotangent()
            total_ref[...] = jnp.zeros_like(total_ref)
            loads[1].wait()
            loads[2].wait()
        for plane, tap, at in TAPS[:5] if stage == 0 else TAPS[5:]:
            start, size = RANGES[plane]
            for image in range(2):
                placed_ref[:, 2 * at + image * size : 2 * at + (image + 1) * size] = dot(
                    grad_ref[image], spread_ref[:, at : at + size], NN, BF
                )
            term = dot(stride_ref[tap], placed_ref[:, 2 * at : 2 * (at + size)], TN)
            for image in range(2):
                total_ref[image, :, start : start + size] += term[:, image * size : (image + 1) * size]
        if stage == 1:
            saves[1].start()
            back_ref[...] = total_ref[...].astype(BF)

    def prepare(rows):
        part_ref[rows] = dot(kernel_ref[:, rows], patches_ref[...], TN)

    def finish(total, rows):
        hidden_ref[rows] = total
        return gate(total).astype(BF)

    inner_exchange(
        nothing,
        prepare,
        lambda j, rows: part_ref[rows, rows_at(j, LANES)],
        finish,
        fill,
        act_ref,
        isbuf,
        irbuf,
        (isend, irecv, isend2, irecv2),
    )
    loads[3].wait()
    joined_phase(
        act_ref, parity_ref, weight_ref, input_ref, place_ref, loads[4], back_ref, joined_ref, pre_ref, backsum_ref,
        moved_ref, *joins,
    )
    for save in saves:
        save.wait()


def second_phase(
    met, weight_ref, joined_ref, back_ref, masked_ref, act_ref, pair, pbuf, mine, sbuf, rbuf, psem, qsem, send, recv,
    send2, recv2, rsend, rrecv,
):
    me, core = lax.axis_index("cin"), lax.axis_index("section")
    sibling = {"section": 1 - core, "cin": me}
    rows = back_ref.shape[0]
    peers = others("cin")
    swaps = []
    for h, (at, size) in enumerate(HALVES):
        span = slice(at, at + size)
        lanes = pl.ds(pl.multiple_of((1 - core) * PIX + at, LANES), size)
        pair[:, span] = dot(weight_ref[...], joined_ref[:, lanes], TN, BF)
        if h == 0:
            met()
        copy = remote(pair.at[:, span], pbuf.at[:, span], psem.at[h], qsem.at[h], sibling)
        copy.start()
        swaps.append(copy)
    first, second = {}, {}
    own = rows_at(me, rows)
    for h, (at, size) in enumerate(HALVES):
        span = slice(at, at + size)
        lanes = pl.ds(pl.multiple_of(core * PIX + at, LANES), size)
        mine[:, span] = dot(weight_ref[...], joined_ref[:, lanes], TN)
        swaps[h].wait_recv()
        for d, peer in enumerate(peers):
            block = rows_at(peer, rows)
            sbuf[d, :, span] = (mine[block, span] + pbuf[block, span].astype(F32)).astype(BF)
            first[h, d] = remote(
                sbuf.at[d, :, span], rbuf.at[d, :, span], send.at[7 * h + d], recv.at[7 * h + d], {"cin": peer}
            )
            first[h, d].start()
    relays = {}
    for h, (at, size) in enumerate(HALVES):
        span = slice(at, at + size)
        lanes = pl.ds(pl.multiple_of(core * PIX + at, LANES), size)
        hidden = mine[own, span] + pbuf[own, span].astype(F32)
        for d in range(7):
            first[h, d].wait_recv()
            hidden = hidden + rbuf[d, :, span].astype(F32)
        masked_ref[own, lanes] = (back_ref[:, span] * slope(hidden)).astype(BF)
        spot = masked_ref.at[own, lanes]
        for d, peer in enumerate(peers):
            second[h, d] = remote(spot, spot, send2.at[7 * h + d], recv2.at[7 * h + d], {"cin": peer})
            second[h, d].start()
        relays[h, 7] = remote(spot, spot, rsend.at[8 * h + 7], rrecv.at[8 * h + 7], sibling)
        relays[h, 7].start()
        act_ref[:, span] = gate(hidden).astype(BF)
    for h, (at, size) in enumerate(HALVES):
        lanes = pl.ds(pl.multiple_of(core * PIX + at, LANES), size)
        for d in range(7):
            spot = masked_ref.at[rows_at(lax.rem(me + 7 - d, 8), rows), lanes]
            second[h, d].wait_recv()
            relays[h, d] = remote(spot, spot, rsend.at[8 * h + d], rrecv.at[8 * h + d], sibling)
            relays[h, d].start()
    for copy in relays.values():
        copy.wait_recv()
    for copy in swaps + list(first.values()) + list(second.values()) + list(relays.values()):
        copy.wait_send()


def input_phase(
    weight_ref, masked_ref, pre_ref, act_ref, joined_ref, place_ref, place_load, out_ref, second_ref, reduce_ref,
    reduce_save, input_ref, sbuf, rbuf, own, send, recv, send2, recv2, send3, recv3, rsend, rrecv,
):
    me, core = lax.axis_index("cout"), lax.axis_index("section")
    line = lax.axis_index("cin")
    rows = pre_ref.shape[0]
    peers = others("cout")
    column_peers, across = column()
    first = []
    for h, (at, size) in enumerate(HALVES):
        span = slice(at, at + size)
        for k in range(4):
            for image in range(2):
                n = k * 2 + image
                mine = (core == image) & (me == core * 4 + k)
                sbuf[n, :, span] = dot(
                    weight_ref[k * rows : (k + 1) * rows, :],
                    masked_ref[:, image * PIX + at : image * PIX + at + size],
                    NN,
                    BF,
                )
                copy = remote(
                    sbuf.at[n, :, span],
                    rbuf.at[me, :, span],
                    send.at[8 * h + n],
                    recv.at[8 * h + me],
                    {"section": image, "cout": core * 4 + k},
                )
                first.append((mine, copy))

                @pl.when(jnp.logical_not(mine))
                def _(copy=copy):
                    copy.start()

                @pl.when(mine)
                def _(n=n, span=span):
                    rbuf[me, :, span] = sbuf[n, :, span]

    def block(source):
        return second_ref.at[rows_at(source, rows), rows_at(core, PIX)]

    def handed(slot, source, src):
        copy = remote(src, block(source), rsend.at[slot], rrecv.at[slot], {"section": 1 - core, "cin": line})
        copy.start()
        return copy

    second_ref[rows_at(line, rows), rows_at(core, PIX)] = act_ref[...]
    third = []
    for d, peer in enumerate(column_peers + [across]):
        copy = remote(act_ref, block(line), send3.at[d], recv3.at[d], {"cin": peer})
        copy.start()
        third.append(copy)
    relays = [handed(7, line, act_ref)]
    reduce_ref[...] = dot(joined_ref[...], masked_ref[...], NT)
    reduce_save.start()
    third[3].wait_recv()
    for d, peer in enumerate(column_peers):
        copy = remote(block(across), block(across), send3.at[4 + d], recv3.at[4 + d], {"cin": peer})
        copy.start()
        third.append(copy)
    relays.append(handed(3, across, block(across)))
    second = []
    for h, (at, size) in enumerate(HALVES):
        span = slice(at, at + size)
        total = jnp.zeros((rows, size), F32)
        for k in range(8):
            arrival = remote(
                sbuf.at[0, :, span],
                rbuf.at[k, :, span],
                send.at[0],
                recv.at[8 * h + k],
                {"section": core, "cout": me},
            )

            @pl.when(jnp.logical_not((me == k) & (me // 4 == core)))
            def _(arrival=arrival):
                arrival.wait_recv()

            total = total + rbuf[k, :, span].astype(F32)
        own[:, span] = (total * slope(pre_ref[:, span])).astype(BF)
        for d, peer in enumerate(peers):
            copy = remote(
                own.at[:, span],
                out_ref.at[rows_at(me, rows), span],
                send2.at[7 * h + d],
                recv2.at[7 * h + d],
                {"cout": peer},
            )
            copy.start()
            second.append(copy)
    out_ref[rows_at(me, rows), :] = own[...]
    place_load.wait()
    input_ref[...] = dot(own[...], place_ref[...], NT, BF)
    base, y = line // 4 * 4, lax.rem(line, 4)
    for d in (0, 1, 2, 4, 5, 6):
        turn = lax.rem(y + 3 - d % 4, 4)
        source = base + turn if d < 3 else 4 - base + turn
        third[d].wait_recv()
        relays.append(handed(d, source, block(source)))
    for copy in second:
        copy.wait_recv()

    def settle():
        for copy in relays:
            copy.wait_recv()
        reduce_save.wait()
        for copy in second + relays + third:
            copy.wait_send()
        for mine, copy in first:

            @pl.when(jnp.logical_not(mine))
            def _(copy=copy):
                copy.wait_send()

    return settle


def last_phase(
    masked_ref, kernel_ref, kernel_load, patches_ref, patches_load, expand_ref, place_ref, place_load, inner_ref,
    local_far, fbuf, ebuf, total_ref, wide, local, near, sbuf, rbuf, send, recv, wsend, wrecv,
):
    me, core = lax.axis_index("cout"), lax.axis_index("section")
    rows = sbuf.shape[1]
    size = masked_ref.shape[0]
    peers = others("cout")
    sibling = {"section": 1 - core, "cout": me}
    swaps = [remote(expand_ref, ebuf, wsend.at[9], wrecv.at[9], sibling)]
    swaps[0].start()
    lane = lax.broadcasted_iota(jnp.int32, (1, PIX), 1)
    kernel_load.wait()
    copies = [
        remote(sbuf.at[peer], rbuf.at[d], send.at[d], recv.at[d], {"cout": peer}) for d, peer in enumerate(peers)
    ]
    for h in range(2):
        span = slice(h * size // 2, (h + 1) * size // 2)
        for tx in range(3):
            for ty in (1, 0, 2):
                dy = ty - 1
                term = dot(kernel_ref[3 * ty + tx, span, :], masked_ref[...], NN)
                if dy:
                    keep = (lane - 32 * dy >= 0) & (lane - 32 * dy < PIX)
                    wide[...] += jnp.where(keep, pltpu.roll(term, (PIX + 32 * dy) % PIX, 1), 0.0)
                else:
                    wide[...] = term
            if tx == 0:
                total_ref[...] = pltpu.roll(wide[...], PIX - 1, 1)
            elif tx == 1:
                total_ref[...] += wide[...]
            else:
                total_ref[...] += pltpu.roll(wide[...], 1, 1)
        for j in range(4):
            sbuf[4 * h + j] = total_ref[j * rows : (j + 1) * rows, :].astype(BF)
        for d, peer in enumerate(peers):

            @pl.when(peer // 4 == h)
            def _(d=d):
                copies[d].start()

    patches_load.wait()
    for t in range(9):
        local[t] = dot(patches_ref[t * size : (t + 1) * size, :], masked_ref[...], NT, BF)
        copy = remote(local.at[t], fbuf.at[t], wsend.at[t], wrecv.at[t], sibling)
        copy.start()
        swaps += [copy, started(local.at[t], local_far.at[t], near.at[t])]
    total = sbuf[me].astype(F32)
    for d in range(7):
        copies[d].wait_recv()
        total = total + rbuf[d].astype(F32)
    high = total.astype(BF)
    rest = total - high.astype(F32)
    middle = rest.astype(BF)
    low = (rest - middle.astype(F32)).astype(BF)
    place_load.wait()
    inner_ref[...] = (
        dot(low, place_ref[...], NT) + dot(middle, place_ref[...], NT) + dot(high, place_ref[...], NT)
    )
    for copy in swaps:
        copy.wait()
    for copy in copies:
        copy.wait_send()


def rear_body(
    reduce_weight_ref, joined_ref, back_ref, pre_ref, place_parity_far, weight_ref, parity_ref, hidden_ref, act_far,
    placed_far, kernel_far, patches_far, place_far,
    reduce_far, own_input_ref, expand_far, stride_far, inner_ref, local_far, fbuf, ebuf,
    second_masked, second_own, place_parity_ref, reduce_ref, input_ref, second_ref, act_ref, placed_ref, kernel_ref,
    patches_ref, place_ref, expand_ref, stride_ref, part, masked_ref, local,
    pair, pbuf, mine, ssbuf, srbuf, psem, qsem, ssend, srecv, ssend2, srecv2, srsend, srrecv,
    jsbuf, jrbuf, jown, jsend, jrecv, jsend2, jrecv2, jsend3, jrecv3, jrsend, jrrecv,
    isbuf, irbuf, isend, irecv, isend2, irecv2, *lasts,
):
    met = signal(all_outer() + [{"cin": p} for p in others("cin")])
    loads = [
        started(far, near, local.at[9 + n])
        for n, (far, near) in enumerate(
            (
                (act_far, act_ref),
                (place_parity_far, place_parity_ref),
                (placed_far, placed_ref),
                (kernel_far, kernel_ref),
                (patches_far, patches_ref),
                (place_far, place_ref),
            )
        )
    ]
    second_phase(
        met, reduce_weight_ref, joined_ref, back_ref, second_masked, second_own, pair, pbuf, mine, ssbuf, srbuf, psem,
        qsem, ssend, srecv, ssend2, srecv2, srsend, srrecv,
    )
    settle = input_phase(
        reduce_weight_ref, second_masked, pre_ref, second_own, joined_ref, place_parity_ref, loads[1], input_ref,
        second_ref, reduce_ref, pltpu.make_async_copy(reduce_ref, reduce_far, local.at[16]), own_input_ref, jsbuf, jrbuf,
        jown, jsend, jrecv, jsend2, jrecv2, jsend3, jrecv3, jrsend, jrrecv,
    )
    saves = []

    def prepare(rows):
        part[rows] = dot(weight_ref[rows], input_ref[...], NN, BF)

    def fill(stage):
        if stage == 0:
            loads[0].wait()
            loads[2].wait()
            expand_ref[...] = dot(act_ref[...], input_ref[...], NT, BF)
            saves.append(started(expand_ref, expand_far, local.at[15]))
            settle()
        for plane, tap, at in TAPS[:4] if stage == 0 else TAPS[4:]:
            start, size = RANGES[plane]
            stride_ref[tap] = (
                dot(placed_ref[:, 2 * at : 2 * at + size], second_ref[:, start : start + size], NT)
                + dot(
                    placed_ref[:, 2 * at + size : 2 * (at + size)],
                    second_ref[:, PIX + start : PIX + start + size],
                    NT,
                )
            ).astype(BF)
            saves.append(started(stride_ref.at[tap], stride_far.at[tap], local.at[tap]))

    def finish(total, rows):
        return (total * slope(hidden_ref[rows])).astype(BF)

    inner_exchange(
        nothing,
        prepare,
        lambda j, rows: dot(part[rows], parity_ref[rows_at(j, LANES), :], NT),
        finish,
        fill,
        masked_ref,
        isbuf,
        irbuf,
        (isend, irecv, isend2, irecv2),
    )
    last_phase(
        masked_ref, kernel_ref, loads[3], patches_ref, loads[4], expand_ref, place_ref, loads[5], inner_ref, local_far,
        fbuf, ebuf, *lasts,
    )
    for save in saves:
        save.wait()


def tail_body(
    stride_ref, first_ref, other_ref, expand_ref, expand_other_ref, reduce_ref, inner_ref, input_ref,
    stride_out, first_out, expand_out, reduce_out, inner_out, input_out,
):
    @pl.when(pl.program_id(0) == 0)
    def _():
        inner_out[...] = inner_ref[...]
        input_out[...] = input_ref[...]
        reduce_out[...] = reduce_ref[...]
        expand_out[...] = expand_ref[...].astype(F32) + expand_other_ref[...].astype(F32)

    stride_out[...] = stride_ref[...].astype(F32)
    first_out[...] = first_ref[...].astype(F32) + other_ref[...].astype(F32)


def tail(stride, first, other, expand, expand_other, reduce, inner, own_input):
    steps = 3

    def tap(array):
        return pl.BlockSpec((array.shape[0] // steps,) + array.shape[1:], lambda t: (t, 0, 0))

    def whole(array):
        return pl.BlockSpec(array.shape, lambda t: (0, 0))

    return pl.pallas_call(
        tail_body,
        grid=(steps,),
        out_shape=(
            jax.ShapeDtypeStruct(stride.shape, F32),
            jax.ShapeDtypeStruct(first.shape, F32),
            jax.ShapeDtypeStruct(expand.shape, F32),
            jax.ShapeDtypeStruct(reduce.shape, F32),
            jax.ShapeDtypeStruct(inner.shape, F32),
            jax.ShapeDtypeStruct(own_input.shape, BF),
        ),
        in_specs=[tap(stride), tap(first), tap(other)]
        + [whole(expand), whole(expand_other), whole(reduce), whole(inner), whole(own_input)],
        out_specs=(tap(stride), tap(first), whole(expand), whole(reduce), whole(inner), whole(own_input)),
        compiler_params=pltpu.CompilerParams(vmem_limit_bytes=56 * 2**20),
    )(stride, first, other, expand, expand_other, reduce, inner, own_input)


def dma(*shape):
    return pltpu.SemaphoreType.DMA(shape)


def vb(*shape):
    return pltpu.VMEM(shape, BF)


def vf(*shape):
    return pltpu.VMEM(shape, F32)


def shards(features, block, first_kernel, expand_weight, reduce_weight, stride_kernel, output_grad):
    channels = first_kernel.shape[1]
    narrow, wide = features.shape[2], block.shape[2]
    outer = stride_kernel.shape[1]
    put_natural = jnp.asarray(place_natural(), BF)
    put_parity = jnp.asarray(place_parity(), BF)
    to_parity = jnp.asarray(natural_to_parity(), BF)

    patches, first_hidden, placed, joined, joined_pre, back_second, act_parity = call(
        front_body,
        [
            ((9 * channels, PIX), BF),
            ((channels, LANES), F32),
            ((channels, 2 * PLACED), BF),
            ((channels, 2 * PIX), BF),
            ((wide, PIX), F32),
            ((wide, PIX), F32),
            ((channels, PIX), BF),
        ],
        [
            vb(TALL, PIX),
            vb(TALL, 512),
            vb(8 * TALL, PIX),
            vb(8 * TALL, 512),
            vf(channels, PIX),
            vf(channels, PIX),
            vb(9 * channels, channels),
            vb(9 * channels, PIX),
            vf(channels, PIX),
            vb(2, channels, 256),
            vb(256, PLACED),
            vb(9, channels, outer),
            vb(channels, 2 * PLACED),
            vb(2, outer, PIX),
            vf(2, outer, PIX),
            vb(PIX, PIX),
            vb(SIDE * SIDE, PIX),
            vb(channels, PIX),
            dma(7),
            dma(14),
            dma(14),
            vb(8, channels, LANES),
            vb(7, channels, LANES),
            dma(14),
            dma(14),
            dma(14),
            dma(14),
            vf(outer, PIX),
            vb(7, wide, PIX),
            vb(7, wide, PIX),
            vb(wide, PIX),
            vb(outer, PIX),
            vb(3, 2, wide, PIX),
            vb(3, 2, wide, PIX),
            vb(wide, PIX),
            vb(wide, PIX),
            dma(14),
            dma(14),
            dma(16),
            dma(16),
            pltpu.SemaphoreType.DMA,
            pltpu.SemaphoreType.DMA,
            dma(4),
            dma(4),
        ],
        0,
        features[0].T,
        output_grad.transpose(0, 2, 1),
        put_natural,
        jnp.asarray(place_grad(), BF),
        first_kernel.reshape(9 * channels, channels),
        jnp.asarray(spread_grad(), BF),
        stride_kernel.transpose(0, 2, 1),
        to_parity,
        expand_weight,
        block[0].T,
        put_parity,
        far_in=(4, 5, 6, 7, 10),
        far_out=(0, 2),
    )

    reduce_local, input_own, expand_local, stride_local, inner_own, first_local, first_other, expand_other = call(
        rear_body,
        [
            (reduce_weight.shape, F32),
            ((wide, SIDE * SIDE), BF),
            (expand_weight.shape, BF),
            ((9, channels, outer), BF),
            ((narrow, SIDE * SIDE), F32),
            ((9, channels, channels), BF),
            ((9, channels, channels), BF),
            (expand_weight.shape, BF),
        ],
        [
            vb(outer, 2 * PIX),
            vb(wide, PIX),
            vb(SIDE * SIDE, PIX),
            vf(*reduce_weight.shape),
            vb(outer, PIX),
            vb(outer, 2 * PIX),
            vb(channels, PIX),
            vb(channels, 2 * PLACED),
            vb(9, channels, channels),
            vb(9 * channels, PIX),
            vb(SIDE * SIDE, PIX),
            vb(*expand_weight.shape),
            vb(9, channels, outer),
            vb(channels, PIX),
            vb(channels, PIX),
            dma(17),
            vb(outer, PIX),
            vb(outer, PIX),
            vf(outer, PIX),
            vb(7, wide, PIX),
            vb(7, wide, PIX),
            dma(2),
            dma(2),
            dma(14),
            dma(14),
            dma(14),
            dma(14),
            dma(16),
            dma(16),
            vb(8, wide, PIX),
            vb(8, wide, PIX),
            vb(wide, PIX),
            dma(16),
            dma(16),
            dma(14),
            dma(14),
            dma(7),
            dma(7),
            dma(8),
            dma(8),
            vb(8, channels, LANES),
            vb(7, channels, LANES),
            dma(14),
            dma(14),
            dma(14),
            dma(14),
            vf(channels // 2, PIX),
            vf(channels // 2, PIX),
            vb(9, channels, channels),
            dma(9),
            vb(8, narrow, PIX),
            vb(7, narrow, PIX),
            dma(7),
            dma(7),
            dma(10),
            dma(10),
        ],
        1,
        reduce_weight,
        joined,
        back_second,
        joined_pre,
        put_parity,
        expand_weight,
        to_parity,
        first_hidden,
        act_parity,
        placed,
        first_kernel,
        patches,
        put_natural,
        far_in=(4, 8, 9, 10, 11, 12),
        far_out=(0, 2, 3, 5, 6, 7),
    )
    stride_gradient, first_gradient, expand_gradient, reduce_gradient, inner_own, input_own = tail(
        stride_local, first_local, first_other, expand_local, expand_other, reduce_local, inner_own, input_own
    )
    return (
        inner_own.T[None],
        input_own.T[None],
        first_gradient,
        expand_gradient,
        reduce_gradient,
        stride_gradient.transpose(0, 2, 1),
    )


def solution(mesh):
    return jax.shard_map(
        shards,
        mesh=mesh,
        in_specs=(
            P("section", None, ("cin", "cout")),
            P("section", None, ("cin", "cout")),
            P(None, "cin", "cout"),
            P("cout", "cin"),
            P(("cin", "section"), "cout"),
            P(None, "cout", ("section", "cin")),
            P(None, None, ("section", "cin", "cout")),
        ),
        out_specs=(
            P("section", None, ("cin", "cout")),
            P("section", None, ("cin", "cout")),
            P(None, "cin", "cout"),
            P("cout", "cin"),
            P(("cin", "section"), "cout"),
            P(None, "cout", ("section", "cin")),
        ),
        check_vma=False,
    )
```
